256 devices in a mesh: req: 64 (over z, x, core), tp: 4 (over y).
Axes of the slice: x: 4, y: 4, z: 8, core: 2. Of those that a mesh axis runs over, the one named last changes fastest.
Arguments:
- tokens_new: bfloat16 [64, 16, 2, 1024], P('req'), may hold values from -6 to 6
- prefix_len: int32 [64], replicated, may hold values from 1 to 4096, as said below
- tail_len: int32 [64, 16], P('req'), may hold values from 1 to 512, as said below
- pool_home: int32 [2048], replicated, may hold values from 0 to 63, as said below
- pool_page: int32 [2048], replicated, may hold values from 0 to 31
- slot_page_cache: bfloat16 [2048, 128, 2, 512], P('req', None, None, 'tp'), may hold values from -64 to 64
- tail_cache: bfloat16 [64, 16, 512, 2, 512], P('req', None, None, None, 'tp'), may hold values from -6 to 6
- routes: int32 [64, 16, 2, 8], P('req'), may hold values from 0 to 31, all different within a row; in each aligned block of 32 rows (0 to 31, 32 to 63, ..., all dimensions but the last counted through in order) at most 12 rows name the same one
- norm_gains: float32 [3, 1024], replicated, may hold values from 0.1 to 1.9
- query_weight: bfloat16 [1024, 1024], P(None, 'tp'), may hold values from -0.1875 to 0.1875
- key_value_weight: bfloat16 [1024, 2, 512], P(None, None, 'tp'), may hold values from -0.1875 to 0.1875
- out_weight: bfloat16 [1024, 1024], P('tp'), may hold values from -0.1875 to 0.1875
- router: bfloat16 [1024, 32], replicated, may hold values from -0.375 to 0.375
- expert_in: bfloat16 [64, 1024, 2, 512], P('req', None, None, 'tp'), as said below
- expert_out: bfloat16 [64, 512, 1024], P('req', 'tp'), as said below
- score_weight: float32 [1024], replicated, may hold values from -0.1875 to 0.1875
Outputs:
- layer_out: bfloat16 [64, 16, 2, 1024], P('req')
- row_score: float32 [64, 16, 2], P('req')
The draws below stay inside these ranges and needn't reach their ends.
Inputs may be any that keep to these rules, and one draw needn't show every extreme that they name: `prefix_len`: some request has exactly 4096 prefix positions. `tail_len`: some sample has exactly 512 tail positions. `pool_home`: entry s * 32 + v describes slot v of the pool of device s of req. Every page 0 to 31 of every request lies in exactly one slot, and one device's pool holds either exactly 1 pages of a request or none of them. `routes`: in the 32 rows of one device no expert is named more than 12 times. `expert_in`: expert table copy c equals copy c mod 32. `expert_out`: expert table copy c equals copy c mod 32.
All inputs are finite; a program needn't handle non-finite values.
Results may differ from the reference program's by a relative error of at most 0.017.
Values may be sent and summed in bfloat16 or wider, within the bound.
A program may use at most 128 MiB of HBM per device.

```python
import math
import jax
import jax.numpy as jnp
import numpy as np
from jax import lax

MODEL_DIM = 1024
QUERY_HEADS = 16
KEY_VALUE_HEADS = 8
HEAD_DIM = 64
FF = 512
EXPERTS = 32
TOPK = 8
SAMPLE_COUNT = 16
NEW_TOKENS = 2
PAGE_POSITIONS = 128
MOST = 12
PLEN = 4096
TAIL_LENGTH = 512
PREFIX_PAGES = 32
PROMPT_COUNT = 64
KEY_VALUE_WIDTH = 512
EXP_SLOTS = 64
N_REQ = 64


def pool_layout(key):
    base_key = jax.random.fold_in(key, 7)
    group_key, slot_key, offset_key, page_key = jax.random.split(base_key, 4)
    home_order = jax.random.permutation(group_key, N_REQ).astype(jnp.int32)
    slot_order = jax.random.permutation(slot_key, PREFIX_PAGES).astype(jnp.int32)
    offset_order = jax.random.permutation(offset_key, N_REQ).astype(jnp.int32)
    page_keys = jax.random.split(page_key, N_REQ)
    page_orders = jax.vmap(lambda single: jax.random.permutation(single, PREFIX_PAGES))(page_keys).astype(jnp.int32)
    offsets = jnp.take(offset_order, slot_order % N_REQ)
    owners = jnp.arange(N_REQ, dtype=jnp.int32)[:, None]
    groups = (owners - offsets[None, :]) % N_REQ
    homes = jnp.take(home_order, groups)
    slot_column = jnp.broadcast_to(jnp.arange(PREFIX_PAGES, dtype=jnp.int32)[None, :], (N_REQ, PREFIX_PAGES))
    prefix_page_list = page_orders[groups, slot_column]
    return (homes.reshape(-1).astype(jnp.int32), prefix_page_list.reshape(-1).astype(jnp.int32))


def draw_pool_home(key, part):
    return pool_layout(key)[0]


def draw_pool_page(key, part):
    return pool_layout(key)[1]


def draw_prefix_len(key, part):
    length_key, spot_key = jax.random.split(jax.random.fold_in(key, 11))
    lengths = jax.random.randint(length_key, (PROMPT_COUNT,), 1, PLEN + 1)
    chosen = jax.random.randint(spot_key, (), 0, PROMPT_COUNT)
    return lengths.at[chosen].set(PLEN).astype(jnp.int32)


def draw_tail_len(key, part):
    length_key, spot_key = jax.random.split(jax.random.fold_in(key, 12))
    lengths = jax.random.randint(length_key, (PROMPT_COUNT * SAMPLE_COUNT,), 1, TAIL_LENGTH + 1)
    chosen = jax.random.randint(spot_key, (), 0, PROMPT_COUNT * SAMPLE_COUNT)
    return lengths.at[chosen].set(TAIL_LENGTH).reshape(PROMPT_COUNT, SAMPLE_COUNT).astype(jnp.int32)


def draw_slot_page_cache(key, part):
    value_key = jax.random.fold_in(jax.random.fold_in(key, 13), 0)
    shape = (N_REQ * PREFIX_PAGES, PAGE_POSITIONS, 2, KEY_VALUE_WIDTH)
    values = jax.random.normal(value_key, shape, jnp.float32)
    return jnp.clip(values, -64.0, 64.0).astype(jnp.bfloat16)


def draw_expert_in(key, part):
    values = jax.random.normal(jax.random.fold_in(key, 17), (EXPERTS, MODEL_DIM, 2, FF), jnp.float32)
    values = jnp.clip(values, -5.0, 5.0) * MODEL_DIM ** (-0.5)
    return jnp.tile(values, (EXP_SLOTS // EXPERTS, 1, 1, 1)).astype(jnp.bfloat16)


def draw_expert_out(key, part):
    values = jax.random.normal(jax.random.fold_in(key, 19), (EXPERTS, FF, MODEL_DIM), jnp.float32)
    values = jnp.clip(values, -5.0, 5.0) * FF ** (-0.5)
    return jnp.tile(values, (EXP_SLOTS // EXPERTS, 1, 1)).astype(jnp.bfloat16)


def levels(rng, dims, cuts, smallest, top_value):
    factor_of = 1.0
    for axis_at, blocks in cuts:
        heights = jax.random.uniform(jax.random.fold_in(jax.random.fold_in(rng, 6), axis_at), (blocks,), jnp.float32, smallest / len(cuts), top_value / len(cuts))
        factor_of = factor_of * jnp.repeat(jnp.exp(heights), dims[axis_at] // blocks).reshape((-1,) + (1,) * (len(dims) - 1 - axis_at))
    return factor_of


def shared_out(key, own, number, rows, count, top, limit, skew):
    sequence = jax.random.permutation(key, count)
    heavy_load, common = shares(count, rows * top, limit, skew, True), shares(count, rows * top, limit, skew, False)
    places = jnp.arange(count)

    def named(sizes, rotation):
        used = int((sizes > 0).sum())
        fixed = max(1, used // 4)
        passed = fixed + (places - fixed + rotation * (used - fixed)) % max(1, count - fixed)
        return jnp.zeros((count,), jnp.int32).at[sequence[jnp.where(places < fixed, places, passed)]].set(jnp.asarray(sizes, jnp.int32))

    sizes = jnp.where(number % 4 == 0, named(heavy_load, number // 4), named(common, number - number // 4 - 1))
    mixed = jax.random.permutation(jax.random.fold_in(own, 3), count)
    source_of, sink = mixed[0:count // 2 * 2:2], mixed[1:count // 2 * 2:2]
    margin = jnp.minimum(sizes[source_of] - 1, limit - sizes[sink]) // 2
    margin = jnp.where((source_of == sequence[0]) | (sink == sequence[0]) | (sizes[sink] == 0), 0, jnp.maximum(margin, 0))
    passed = jax.random.randint(jax.random.fold_in(own, 4), (count // 2,), 0, 1 << 20) % (margin + 1)
    sizes = sizes.at[source_of].add(-passed).at[sink].add(passed)
    members = jnp.searchsorted(jnp.cumsum(sizes), jnp.arange(rows * top), side="right").astype(jnp.int32)
    grid = members.reshape(top, rows).T
    grid = grid[jax.random.permutation(jax.random.fold_in(own, 1), rows)]
    rotation = jax.random.randint(jax.random.fold_in(own, 2), (rows, 1), 0, top)
    return jnp.take_along_axis(grid, (jnp.arange(top)[None, :] + rotation) % top, axis=1)


def shares(number_of, total, reach, lean, full):
    loads = [(1 << 20) // math.isqrt(standing ** lean) + 1 for standing in range(1, number_of + 1)]
    largest = reach if full else min(reach, max(-(-total // number_of), total * loads[0] // sum(loads)))
    least = 1 if total - largest >= number_of - 1 else 0
    given, spare = [largest] + [least] * (number_of - 1), total - largest - least * (number_of - 1)
    while spare > 0:
        movable = [i for i in range(1, number_of) if given[i] < largest] or [i for i in range(1, number_of) if given[i] < reach]
        pool, budget = sum([loads[i] for i in movable]), spare
        for i in movable:
            extra = min(reach - given[i], max(1, budget * loads[i] // pool), spare)
            given[i] = given[i] + extra
            spare = spare - extra
    return np.array(given)


def scatter_about(own_key, dims, scale, limit, cuts=(), kind=jnp.bfloat16):
    loudness = levels(own_key, dims, cuts, -0.22, 0.18) if cuts else 1.0
    drawn = jax.random.normal(own_key, dims, jnp.float32) * scale * loudness
    return jnp.minimum(jnp.maximum(drawn, -limit), limit).astype(kind)


def setup_inputs(seed: int = 0) -> dict:
    streams_of = jax.random.split(jax.random.key(seed), 17)
    tokens_new = scatter_about(streams_of[0], (PROMPT_COUNT, SAMPLE_COUNT, NEW_TOKENS, MODEL_DIM), 1.0, 6.0, ((0, 64),))
    prefix_len = draw_prefix_len(jax.random.fold_in(streams_of[16], 71), 0)
    tail_len = draw_tail_len(jax.random.fold_in(streams_of[16], 71), 0)
    pool_home = draw_pool_home(jax.random.fold_in(streams_of[16], 71), 0)
    pool_page = draw_pool_page(jax.random.fold_in(streams_of[16], 71), 0)
    slot_page_cache = draw_slot_page_cache(jax.random.fold_in(streams_of[16], 71), 0)
    tail_cache = scatter_about(streams_of[6], (PROMPT_COUNT, SAMPLE_COUNT, TAIL_LENGTH, 2, KEY_VALUE_WIDTH), 1.0, 6.0, ((0, 64), (4, 4)))
    routes_keys = jax.random.split(jax.random.fold_in(streams_of[7], 1), PROMPT_COUNT * SAMPLE_COUNT * NEW_TOKENS // (SAMPLE_COUNT * NEW_TOKENS))
    routes_turns = jax.random.permutation(jax.random.fold_in(streams_of[7], 3), PROMPT_COUNT * SAMPLE_COUNT * NEW_TOKENS // (SAMPLE_COUNT * NEW_TOKENS))
    routes = jax.vmap(lambda own, number: shared_out(jax.random.fold_in(streams_of[7], 2), own, number, SAMPLE_COUNT * NEW_TOKENS, EXPERTS, TOPK, MOST, 2))(routes_keys, routes_turns).reshape((PROMPT_COUNT, SAMPLE_COUNT, NEW_TOKENS, TOPK))
    norm_gains = jnp.clip(1.0 + 0.18 * jax.random.normal(streams_of[8], (3, MODEL_DIM), jnp.float32), 0.1, 1.9)
    query_weight = scatter_about(streams_of[9], (MODEL_DIM, QUERY_HEADS * HEAD_DIM), MODEL_DIM ** -0.5, 0.1875, ((1, 4),))
    key_value_weight = scatter_about(streams_of[10], (MODEL_DIM, 2, KEY_VALUE_WIDTH), MODEL_DIM ** -0.5, 0.1875, ((2, 4),))
    out_weight = scatter_about(streams_of[11], (QUERY_HEADS * HEAD_DIM, MODEL_DIM), (QUERY_HEADS * HEAD_DIM) ** -0.5, 0.1875, ((0, 4),))
    router = scatter_about(streams_of[12], (MODEL_DIM, EXPERTS), (MODEL_DIM // 4) ** -0.5, 0.375)
    expert_in = draw_expert_in(jax.random.fold_in(streams_of[16], 71), 0)
    expert_out = draw_expert_out(jax.random.fold_in(streams_of[16], 71), 0)
    score_weight = scatter_about(streams_of[15], (MODEL_DIM,), MODEL_DIM ** -0.5, 0.1875, (), jnp.float32)
    return dict(tokens_new=tokens_new, prefix_len=prefix_len, tail_len=tail_len, pool_home=pool_home, pool_page=pool_page, slot_page_cache=slot_page_cache, tail_cache=tail_cache, routes=routes, norm_gains=norm_gains, query_weight=query_weight, key_value_weight=key_value_weight, out_weight=out_weight, router=router, expert_in=expert_in, expert_out=expert_out, score_weight=score_weight)


EPSILON = 1e-05
ROPE_BASE = 10000.0
LOWEST = -1e+30

def rms_scale(values, gain_row):
    widened = values.astype(jnp.float32)
    return widened * lax.rsqrt(lax.optimization_barrier(jnp.mean(widened * widened, axis=-1, keepdims=True)) + EPSILON) * gain_row

def apply_rotary(vectors, token_positions):
    half_width = vectors.shape[-1] // 2
    frequency = ROPE_BASE ** (-jnp.arange(half_width, dtype=jnp.float32) / half_width)
    angles = token_positions.astype(jnp.float32)[..., None] * frequency
    cosine = jnp.cos(angles)[..., None, :]
    sine_part = jnp.sin(angles)[..., None, :]
    leading = vectors[..., :half_width]
    trailing = vectors[..., half_width:]
    return jnp.concatenate([leading * cosine - trailing * sine_part, trailing * cosine + leading * sine_part], axis=-1)

def block_stats(scores, visible):
    block_top = lax.optimization_barrier(jnp.max(jnp.where(visible, scores, LOWEST), axis=-1))
    weights = jnp.where(visible, jnp.exp(jnp.where(visible, scores - block_top[..., None], 0.0)), 0.0)
    return (block_top, lax.optimization_barrier(jnp.sum(weights, axis=-1)), weights)

def rounded(values):
    return lax.optimization_barrier(values.astype(jnp.bfloat16)).astype(jnp.float32)

def attend(query_rows, fresh_keys, fresh_values, prefix_page_list, page_ids, prefix_count, sample_tails, tail_count):
    score_scale = HEAD_DIM ** (-0.5)
    query_wide = query_rows.astype(jnp.float32)
    page_keys = prefix_page_list[:, :, 0].astype(jnp.float32)
    page_values = prefix_page_list[:, :, 1].astype(jnp.float32)
    page_scores = jnp.einsum('sikgd,btkd->bsikgt', query_wide, page_keys) * score_scale
    page_spots = page_ids[:, None] * PAGE_POSITIONS + jnp.arange(PAGE_POSITIONS, dtype=jnp.int32)[None, :]
    page_seen = ((page_spots < prefix_count) & (page_ids[:, None] >= 0))[:, None, None, None, None, :]
    page_top, page_total, page_weights = block_stats(page_scores, page_seen)
    page_numer = jnp.einsum('bsikgt,btkd->bsikgd', rounded(page_weights), page_values)
    tail_block_list = sample_tails.reshape(SAMPLE_COUNT, TAIL_LENGTH // PAGE_POSITIONS, PAGE_POSITIONS, 2, KEY_VALUE_HEADS, HEAD_DIM).astype(jnp.float32)
    tail_scores = jnp.einsum('sikgd,sbtkd->sbikgt', query_wide, tail_block_list[:, :, :, 0]) * score_scale
    tail_spots = jnp.arange(TAIL_LENGTH, dtype=jnp.int32).reshape(TAIL_LENGTH // PAGE_POSITIONS, PAGE_POSITIONS)
    tail_seen = (tail_spots[None] < tail_count[:, None, None])[:, :, None, None, None, :]
    tail_top, tail_total, tail_weights = block_stats(tail_scores, tail_seen)
    tail_numer = jnp.einsum('sbikgt,sbtkd->sbikgd', rounded(tail_weights), tail_block_list[:, :, :, 1])
    fresh_scores = jnp.einsum('sikgd,sjkd->sikgj', query_wide, fresh_keys.astype(jnp.float32)) * score_scale
    fresh_seen = (jnp.arange(NEW_TOKENS)[None, :] <= jnp.arange(NEW_TOKENS)[:, None])[None, :, None, None, :]
    fresh_top, fresh_total, fresh_weights = block_stats(fresh_scores, fresh_seen)
    fresh_numer = jnp.einsum('sikgj,sjkd->sikgd', rounded(fresh_weights), fresh_values.astype(jnp.float32))
    overall = jnp.maximum(jnp.maximum(lax.optimization_barrier(jnp.max(page_top, axis=0)), lax.optimization_barrier(jnp.max(tail_top, axis=1))), fresh_top)
    page_factor = jnp.exp(page_top - overall[None])
    tail_factor = jnp.exp(tail_top - overall[:, None])
    fresh_factor = jnp.exp(fresh_top - overall)
    denominator = lax.optimization_barrier(jnp.sum(page_factor * page_total, axis=0)) + lax.optimization_barrier(jnp.sum(tail_factor * tail_total, axis=1)) + fresh_factor * fresh_total
    numerator = lax.optimization_barrier(jnp.sum(page_factor[..., None] * page_numer, axis=0)) + lax.optimization_barrier(jnp.sum(tail_factor[..., None] * tail_numer, axis=1)) + fresh_factor[..., None] * fresh_numer
    return numerator / denominator[..., None]

def reference(tokens_new, prefix_len, tail_len, pool_home, pool_page, slot_page_cache, tail_cache, routes, norm_gains, query_weight, key_value_weight, out_weight, router, expert_in, expert_out, score_weight):
    row_count = PROMPT_COUNT * SAMPLE_COUNT * NEW_TOKENS
    query_group_width = QUERY_HEADS // KEY_VALUE_HEADS
    flat_tokens = tokens_new.reshape(row_count, MODEL_DIM)
    normalized_input = rms_scale(flat_tokens, norm_gains[0]).astype(jnp.bfloat16)
    query_vectors = jnp.dot(normalized_input, query_weight, preferred_element_type=jnp.float32).reshape(PROMPT_COUNT, SAMPLE_COUNT, NEW_TOKENS, QUERY_HEADS, HEAD_DIM)
    key_value_rows = jnp.dot(normalized_input, key_value_weight.reshape(MODEL_DIM, 2 * KEY_VALUE_WIDTH), preferred_element_type=jnp.float32).reshape(PROMPT_COUNT, SAMPLE_COUNT, NEW_TOKENS, 2, KEY_VALUE_HEADS, HEAD_DIM)
    token_positions = prefix_len[:, None, None] + tail_len[:, :, None] + jnp.arange(NEW_TOKENS, dtype=jnp.int32)[None, None, :]
    rotated_query = apply_rotary(query_vectors, token_positions).astype(jnp.bfloat16).reshape(PROMPT_COUNT, SAMPLE_COUNT, NEW_TOKENS, KEY_VALUE_HEADS, query_group_width, HEAD_DIM)
    key_rot = apply_rotary(key_value_rows[:, :, :, 0], token_positions).astype(jnp.bfloat16)
    value_new = key_value_rows[:, :, :, 1].astype(jnp.bfloat16)

    def one_prompt(prompt):
        score_ranking = jnp.argsort(jnp.where(pool_home == prompt, pool_page, PREFIX_PAGES), stable=True)[:PREFIX_PAGES].astype(jnp.int32)
        prefix_page_list = jnp.take(slot_page_cache, score_ranking, axis=0).reshape(PREFIX_PAGES, PAGE_POSITIONS, 2, KEY_VALUE_HEADS, HEAD_DIM)
        page_ids = jnp.take(pool_page, score_ranking)
        return attend(rotated_query[prompt], key_rot[prompt], value_new[prompt], prefix_page_list, page_ids, prefix_len[prompt], tail_cache[prompt], tail_len[prompt])
    attention = lax.map(one_prompt, jnp.arange(PROMPT_COUNT, dtype=jnp.int32))
    attn_rows = attention.reshape(row_count, QUERY_HEADS * HEAD_DIM).astype(jnp.bfloat16)
    attn_out = jnp.dot(attn_rows, out_weight, preferred_element_type=jnp.float32)
    residual = (flat_tokens.astype(jnp.float32) + attn_out).astype(jnp.bfloat16)
    normed_moe = rms_scale(residual, norm_gains[1]).astype(jnp.bfloat16)
    logits = jnp.dot(normed_moe, router, preferred_element_type=jnp.float32)
    routing = routes.reshape(row_count, TOPK)
    gate_values = jax.nn.softmax(jnp.take_along_axis(logits, routing, axis=1), axis=-1)
    pair_expert = routing.reshape(-1)
    pair_gate = gate_values.reshape(-1)
    pair_token = jnp.arange(row_count * TOPK, dtype=jnp.int32) // TOPK
    capacity = N_REQ * MOST

    def one_expert(expert):
        score_ranking = jnp.argsort((pair_expert != expert).astype(jnp.int32), stable=True)[:capacity].astype(jnp.int32)
        chosen = jnp.take(pair_token, score_ranking)
        inputs = jnp.take(normed_moe, chosen, axis=0)
        gate_up = jnp.dot(inputs, expert_in[expert].reshape(MODEL_DIM, 2 * FF), preferred_element_type=jnp.float32).reshape(capacity, 2, FF)
        hidden = (jax.nn.silu(gate_up[:, 0]) * gate_up[:, 1]).astype(jnp.bfloat16)
        result = jnp.dot(hidden, expert_out[expert], preferred_element_type=jnp.float32)
        weight = jnp.where(jnp.take(pair_expert, score_ranking) == expert, jnp.take(pair_gate, score_ranking), 0.0)
        return (result * weight[:, None], chosen)
    results, chosen_rows = lax.map(one_expert, jnp.arange(EXPERTS, dtype=jnp.int32))
    expert_mix = jnp.zeros((row_count, MODEL_DIM), jnp.float32).at[chosen_rows.reshape(-1)].add(results.reshape(-1, MODEL_DIM))
    layer_out = (residual.astype(jnp.float32) + expert_mix).astype(jnp.bfloat16)
    final_norm = rms_scale(layer_out, norm_gains[2])
    row_score = lax.optimization_barrier(jnp.sum(final_norm * score_weight, axis=-1))
    return (layer_out.reshape(PROMPT_COUNT, SAMPLE_COUNT, NEW_TOKENS, MODEL_DIM), row_score.reshape(PROMPT_COUNT, SAMPLE_COUNT, NEW_TOKENS))
```

```python
import jax
import jax.numpy as jnp
from jax import lax
from jax.experimental import pallas as pl
from jax.experimental.pallas import tpu as pltpu
from jax.sharding import PartitionSpec as P

HEAD_DIM = 64
MOST = 12


EPSILON = 1e-05
ROPE_BASE = 10000.0
LOWEST = -1e30


def rms_scale(values, gain_row):
    widened = values.astype(jnp.float32)
    return (
        widened
        * lax.rsqrt(jnp.mean(widened * widened, axis=-1, keepdims=True) + EPSILON)
        * gain_row
    )


def apply_rotary(vectors, token_positions):
    half_width = vectors.shape[-1] // 2
    frequency = ROPE_BASE ** (-jnp.arange(half_width, dtype=jnp.float32) / half_width)
    angles = token_positions.astype(jnp.float32)[..., None] * frequency
    cosine = jnp.cos(angles)[..., None, :]
    sine_part = jnp.sin(angles)[..., None, :]
    leading = vectors[..., :half_width]
    trailing = vectors[..., half_width:]
    return jnp.concatenate(
        [leading * cosine - trailing * sine_part, trailing * cosine + leading * sine_part], axis=-1
    )


def block_stats(scores, visible):
    block_top = jnp.max(jnp.where(visible, scores, LOWEST), axis=-1)
    weights = jnp.where(
        visible, jnp.exp(jnp.where(visible, scores - block_top[..., None], 0.0)), 0.0
    )
    return (block_top, jnp.sum(weights, axis=-1), weights.astype(jnp.bfloat16))


MESH = pl.DeviceIdType.MESH
F32 = jnp.float32
BF16 = jnp.bfloat16


def iota(shape, dim):
    return lax.broadcasted_iota(jnp.int32, shape, dim)


def mm(a, b):
    return lax.dot_general(a, b, (((1,), (0,)), ((), ())), preferred_element_type=F32)


def mm_t(a, b):
    return lax.dot_general(a, b, (((1,), (1,)), ((), ())), preferred_element_type=F32)


def remote(src, dst, send_sem, recv_sem, req, tp):
    return pltpu.make_async_remote_copy(
        src_ref=src,
        dst_ref=dst,
        send_sem=send_sem,
        recv_sem=recv_sem,
        device_id=(req, tp),
        device_id_type=MESH,
    )


def spread_halves(values):
    high = values.astype(BF16)
    return high, (values - high.astype(F32)).astype(BF16)


def deinterleave(src_ref, dst_ref):
    row = iota((256, 256), 0)
    pick = (iota((256, 256), 1) == 2 * (row % 128) + row // 128).astype(BF16)
    for block in range(src_ref.shape[0] // 256):
        both = mm(pick, src_ref[pl.ds(block * 256, 256), :]).astype(BF16)
        dst_ref[pl.ds(block * 128, 128), 0:128] = both[:128]
        dst_ref[pl.ds(block * 128, 128), 128:256] = both[128:]


def rms(values, gain):
    return values * lax.rsqrt(jnp.mean(values * values, axis=-1, keepdims=True) + EPSILON) * gain


def exchange_start(slots, send_sem, recv_sem, req, tp):
    for step in (1, 3, 2):
        remote(
            slots.at[tp], slots.at[tp], send_sem.at[step], recv_sem.at[tp], req, (tp + step) % 4
        ).start()


def exchange_finish(slots, send_sem, recv_sem, req, tp):
    for step in (1, 3, 2):
        other = (tp + step) % 4
        copy = remote(slots.at[tp], slots.at[other], send_sem.at[step], recv_sem.at[other], req, other)
        copy.wait_recv()
    for step in (1, 3, 2):
        copy = remote(slots.at[tp], slots.at[tp], send_sem.at[step], recv_sem.at[tp], req, tp)
        copy.wait_send()
    return (
        slots[0].astype(F32) + slots[1].astype(F32) + slots[2].astype(F32) + slots[3].astype(F32)
    )


def route_tables(routes):
    column = iota((32, 32), 1)
    uses = jnp.zeros((32, 32), F32)
    for k in range(8):
        uses = uses + (routes[:, k : k + 1] == column).astype(F32)
    earlier = (iota((32, 32), 0) > column).astype(BF16)
    rank = mm(earlier, uses.astype(BF16))
    return uses, jnp.where(uses > 0, rank, -1.0).astype(BF16)


def spread_matrices(rank):
    repeat = (iota((256, 32), 0) // 8 == iota((256, 32), 1)).astype(BF16)
    slot = (iota((256, 32), 0) % 8).astype(F32)
    whole = (mm_t(repeat, rank) == slot).astype(F32).astype(BF16)
    slot2 = iota((256, 64), 0) % 8
    at_half = mm_t(repeat, jnp.concatenate([rank, rank], axis=0))
    half = (
        jnp.where(iota((256, 64), 1) // 32 == slot2 // 4, at_half, -1.0)
        == (8 + slot2 % 4).astype(F32)
    )
    return whole, half.astype(F32).astype(BF16)


def combine_matrices(rank, gates):
    repeat = (iota((256, 32), 0) // 8 == iota((256, 32), 1)).astype(BF16)
    at = mm_t(rank, repeat)
    gate_parts = [mm_t(part, repeat) for part in spread_halves(gates)]
    slot = iota((32, 256), 1) % 8
    chosen = [at == slot.astype(F32)]
    for h in range(2):
        chosen.append(jnp.where(slot // 4 == h, at, -1.0) == (8 + slot % 4).astype(F32))
    return [[jnp.where(pick, part, 0.0).astype(BF16) for part in gate_parts] for pick in chosen]


def moe_stage(req, tp, residual, routes_ref, gains_ref, router_ref, eout_ref, score_ref,
              out_ref, row_score_ref, win, out_buf, in_buf, ret_buf, back_buf, mix_slots,
              dsend, drecv, rsend, rrecv, lsem, msend, mrecv):
    z = req // 8
    xc = req % 8
    core = req % 2
    far = jnp.where(core == 0, 2, 6)
    hops = (0, 1, 7, far)

    uses, rank = route_tables(routes_ref[...])
    whole, half = spread_matrices(rank)
    normed = rms(residual.astype(F32), gains_ref[1:2, :]).astype(BF16)
    out_buf[:, :, 0:1024] = mm(whole, normed).reshape(32, 8, 1024).astype(BF16)
    stacked = jnp.concatenate([normed[:, :512], normed[:, 512:]], axis=0)
    out_buf[:, :, 1024:1536] = mm(half, stacked).reshape(32, 8, 512).astype(BF16)

    for g in (3, 2, 1, 0):
        to_z = (z + hops[g]) % 8
        base = (to_z % 4) * 8

        @pl.loop(1, 8)
        def _(i):
            other = (xc + i) % 8
            remote(
                out_buf.at[base + other], in_buf.at[g, xc], dsend.at[g, i], drecv.at[g, xc],
                to_z * 8 + other, tp,
            ).start()

        if g == 0:
            pltpu.make_async_copy(out_buf.at[base + xc], in_buf.at[0, xc], lsem.at[0]).start()
        else:
            remote(
                out_buf.at[base + xc], in_buf.at[g, xc], dsend.at[g, 0], drecv.at[g, xc],
                to_z * 8 + xc, tp,
            ).start()

    logits = mm_t(normed, router_ref[...])
    shown = jnp.where(uses > 0, logits, LOWEST)
    weights = jnp.where(uses > 0, jnp.exp(shown - jnp.max(shown, axis=-1, keepdims=True)), 0.0)
    gates = weights / jnp.sum(weights, axis=-1, keepdims=True)
    combine = combine_matrices(rank, gates)

    own_expert = (z % 4) * 8 + xc
    backs = (0, 7, 1, (8 - far) % 8)
    upper = iota((64, 1), 0) % 8 < 4

    for g in range(4):
        def from_z(other):
            if g < 3:
                return (z + backs[g]) % 8
            return (z + jnp.where(other % 2 == 0, 6, 2)) % 8

        if g == 0:
            pltpu.make_async_copy(out_buf.at[own_expert], in_buf.at[0, xc], lsem.at[0]).wait()

        @pl.loop(1 if g == 0 else 0, 8)
        def _(i):
            other = (xc + i) % 8
            remote(
                out_buf.at[0], in_buf.at[g, other], dsend.at[g, i], drecv.at[g, other], req, tp
            ).wait_recv()

        rows = in_buf[g].astype(F32)
        rows_a = rows[:, :, :1024].reshape(64, 1024).astype(BF16)
        rows_b = rows[:, :, 1024:].reshape(64, 512).astype(BF16)
        up_a = mm(rows_a, win[...])
        low = mm(rows_b, win[0:512, :])
        high = mm(rows_b, win[512:1024, :])
        mine = jnp.where(upper, low, high)
        swapped = jnp.where(upper, pltpu.roll(mine, 60, 0), pltpu.roll(mine, 4, 0))
        up_b = mine + swapped
        both = jnp.concatenate([up_a, up_b], axis=0)
        gate = both[:, :128]
        hidden = (gate / (1.0 + jnp.exp(-gate)) * both[:, 128:]).astype(BF16)
        result = mm(hidden, eout_ref[...])
        ret_buf[g, :, :, 0:1024] = result[:64].reshape(8, 8, 1024).astype(BF16)
        second = result[64:]
        ret_buf[g, :, :, 1024:1536] = (
            jnp.where(upper, second[:, :512], second[:, 512:]).reshape(8, 8, 512).astype(BF16)
        )

        if g == 0:
            pltpu.make_async_copy(ret_buf.at[0, xc], back_buf.at[own_expert], lsem.at[1]).start()

        @pl.loop(1 if g == 0 else 0, 8)
        def _(i):
            other = (xc + i) % 8
            remote(
                ret_buf.at[g, other], back_buf.at[own_expert], rsend.at[g, i],
                rrecv.at[own_expert], from_z(other) * 8 + other, tp,
            ).start()

    pltpu.make_async_copy(ret_buf.at[0, xc], back_buf.at[own_expert], lsem.at[1]).wait()

    @pl.loop(1, 32)
    def _(i):
        expert = (own_expert + i) % 32
        remote(
            ret_buf.at[0, 0], back_buf.at[expert], rsend.at[0, 0], rrecv.at[expert], req, tp
        ).wait_recv()

    back = back_buf[...].astype(F32)
    back_a = back[:, :, :1024].reshape(256, 1024).astype(BF16)
    back_b = back[:, :, 1024:].reshape(256, 512).astype(BF16)
    mix_b = [mm(combine[1 + h][0], back_b) + mm(combine[1 + h][1], back_b) for h in range(2)]
    mix = mm(combine[0][0], back_a) + mm(combine[0][1], back_a)
    mix = mix + jnp.concatenate(mix_b, axis=1)
    mix_slots[tp] = mix.astype(BF16)
    exchange_start(mix_slots, msend, mrecv, req, tp)

    for g in range(4):

        @pl.loop(1 if g == 0 else 0, 8)
        def _(i):
            remote(
                out_buf.at[0], in_buf.at[g, 0], dsend.at[g, i], drecv.at[g, 0], req, tp
            ).wait_send()
            remote(
                ret_buf.at[g, 0], back_buf.at[0], rsend.at[g, i], rrecv.at[0], req, tp
            ).wait_send()

    expert_mix = exchange_finish(mix_slots, msend, mrecv, req, tp)
    layer_out = (residual.astype(F32) + expert_mix).astype(BF16)
    out_ref[...] = layer_out
    final = rms(layer_out.astype(F32), gains_ref[2:3, :])
    row_score_ref[...] = jnp.sum(final * score_ref[...], axis=-1, keepdims=True)


def moe_scratch():
    dma = pltpu.SemaphoreType.DMA
    return [
        pltpu.VMEM((1024, 256), BF16),
        pltpu.VMEM((32, 8, 1536), BF16),
        pltpu.VMEM((4, 8, 8, 1536), BF16),
        pltpu.VMEM((4, 8, 8, 1536), BF16),
        pltpu.VMEM((32, 8, 1536), BF16),
        pltpu.VMEM((4, 32, 1024), BF16),
        dma((4, 8)),
        dma((4, 8)),
        dma((4, 8)),
        dma((32,)),
        dma((2,)),
        dma((4,)),
        dma((4,)),
    ]


def moe_kernel(tok_ref, part_ref, routes_ref, gains_ref, router_ref, ein_ref, eout_ref, score_ref,
               out_ref, row_score_ref, attn_slots, asend, arecv, win, *rest):
    req = lax.axis_index("req")
    tp = lax.axis_index("tp")
    z = req // 8
    xc = req % 8
    barrier = pltpu.get_barrier_semaphore()
    for step in (1, 2, 3):
        pl.semaphore_signal(barrier, 1, device_id=(req, (tp + step) % 4), device_id_type=MESH)

    @pl.loop(1, 40)
    def _(i):
        other = ((z + 6 + (i // 8 + 2) % 5) % 8) * 8 + (xc + i) % 8
        pl.semaphore_signal(barrier, 1, device_id=(other, tp), device_id_type=MESH)

    attn_slots[tp] = part_ref[...].astype(BF16)
    pl.semaphore_wait(barrier, 42)
    exchange_start(attn_slots, asend, arecv, req, tp)
    deinterleave(ein_ref, win)
    attn_out = exchange_finish(attn_slots, asend, arecv, req, tp)
    residual = (tok_ref[...].astype(F32) + attn_out).astype(BF16)
    moe_stage(req, tp, residual, routes_ref, gains_ref, router_ref, eout_ref, score_ref,
              out_ref, row_score_ref, win, *rest)


def moe_call(flat_tokens, attn_part, routing, norm_gains, router, expert_in, expert_out, score_weight):
    dma = pltpu.SemaphoreType.DMA
    vmem = pl.BlockSpec(memory_space=pltpu.VMEM)
    return pl.pallas_call(
        moe_kernel,
        out_shape=(
            jax.ShapeDtypeStruct((32, 1024), BF16),
            jax.ShapeDtypeStruct((32, 1), F32),
        ),
        in_specs=[vmem] * 8,
        out_specs=(vmem, vmem),
        scratch_shapes=[pltpu.VMEM((4, 32, 1024), BF16), dma((4,)), dma((4,))] + moe_scratch(),
        compiler_params=pltpu.CompilerParams(
            collective_id=0, has_side_effects=True, vmem_limit_bytes=48 * 1024 * 1024
        ),
    )(flat_tokens, attn_part, routing, norm_gains, router.T, expert_in.reshape(2048, 128),
      expert_out[0], score_weight[None])


def shards(
    tokens_new,
    prefix_len,
    tail_len,
    pool_home,
    pool_page,
    slot_page_cache,
    tail_cache,
    routes,
    norm_gains,
    query_weight,
    key_value_weight,
    out_weight,
    router,
    expert_in,
    expert_out,
    score_weight,
):
    device = lax.axis_index("req")
    req_count = lax.axis_size("req")
    samples = tokens_new.shape[1]
    fresh_count = tokens_new.shape[2]
    model_width = tokens_new.shape[3]
    row_count = samples * fresh_count
    head_count = query_weight.shape[1] // HEAD_DIM
    kv_heads = key_value_weight.shape[2] // HEAD_DIM
    query_group_width = head_count // kv_heads
    pool_slots = slot_page_cache.shape[0]
    page_size = slot_page_cache.shape[1]
    slot_cap = max(1, pool_slots // req_count)
    score_scale = HEAD_DIM ** (-0.5)
    flat_tokens = tokens_new.reshape(row_count, model_width)
    normalized_input = rms_scale(flat_tokens, norm_gains[0]).astype(jnp.bfloat16)
    query_vectors = jnp.dot(
        normalized_input, query_weight, preferred_element_type=jnp.float32
    ).reshape(samples, fresh_count, head_count, HEAD_DIM)
    key_value_rows = jnp.dot(
        normalized_input,
        key_value_weight.reshape(model_width, 2 * kv_heads * HEAD_DIM),
        preferred_element_type=jnp.float32,
    ).reshape(samples, fresh_count, 2, kv_heads, HEAD_DIM)
    own_length = jnp.take(prefix_len, device)
    token_positions = (
        own_length + tail_len[0][:, None] + jnp.arange(fresh_count, dtype=jnp.int32)[None, :]
    )
    rotated_query = (
        apply_rotary(query_vectors, token_positions)
        .astype(jnp.bfloat16)
        .reshape(samples, fresh_count, kv_heads, query_group_width, HEAD_DIM)
    )
    key_rot = apply_rotary(key_value_rows[:, :, 0], token_positions).astype(jnp.bfloat16)
    value_new = key_value_rows[:, :, 1].astype(jnp.bfloat16)
    owner_homes = pool_home.reshape(req_count, pool_slots)
    owner_pages = pool_page.reshape(req_count, pool_slots)
    own_home = jnp.take(owner_homes, device, axis=0)
    slot_range = jnp.arange(pool_slots, dtype=jnp.int32)
    cap_range = jnp.arange(slot_cap, dtype=jnp.int32)
    same_home = own_home[:, None] == own_home[None, :]
    earlier = slot_range[:, None] <= slot_range[None, :]
    slot_rank = jnp.sum((same_home & earlier).astype(jnp.int32), axis=0)
    picked_slots = (
        own_home[None, None, :] == jnp.arange(req_count, dtype=jnp.int32)[:, None, None]
    ) & (slot_rank[None, None, :] == cap_range[None, :, None] + 1)
    slot_index = jnp.sum(
        picked_slots.astype(jnp.int32) * slot_range[None, None, :], axis=-1
    ).reshape(-1)
    page_range = jnp.arange(page_size, dtype=jnp.int32)
    outgoing = jnp.take(slot_page_cache, slot_index, axis=0).reshape(
        (req_count, slot_cap) + slot_page_cache.shape[1:]
    )
    arrived = lax.all_to_all(outgoing, "req", split_axis=0, concat_axis=0, tiled=True)
    home_match = owner_homes == device
    home_rank = jnp.cumsum(home_match.astype(jnp.int32), axis=1)
    wanted = home_match[:, None, :] & (home_rank[:, None, :] == cap_range[None, :, None] + 1)
    page_ids = jnp.where(
        jnp.any(wanted, axis=-1),
        jnp.sum(wanted.astype(jnp.int32) * owner_pages[:, None, :], axis=-1),
        -1,
    ).reshape(-1)
    blocks = arrived.reshape(req_count * slot_cap, page_size, 2, kv_heads, HEAD_DIM)
    page_scores = (
        jnp.einsum(
            "sikgd,btkd->bsikgt", rotated_query, blocks[:, :, 0], preferred_element_type=jnp.float32
        )
        * score_scale
    )
    page_spots = page_ids[:, None] * page_size + page_range[None, :]
    page_seen = ((page_spots < own_length) & (page_ids[:, None] >= 0))[:, None, None, None, None, :]
    page_top, page_total, page_weights = block_stats(page_scores, page_seen)
    page_numer = jnp.einsum(
        "bsikgt,btkd->bsikgd", page_weights, blocks[:, :, 1], preferred_element_type=jnp.float32
    )
    tail_count = tail_cache.shape[2]
    tail_block_list = tail_cache[0].reshape(
        samples, tail_count // page_size, page_size, 2, kv_heads, HEAD_DIM
    )
    tail_scores = (
        jnp.einsum(
            "sikgd,sbtkd->sbikgt",
            rotated_query,
            tail_block_list[:, :, :, 0],
            preferred_element_type=jnp.float32,
        )
        * score_scale
    )
    tail_spots = jnp.arange(tail_count, dtype=jnp.int32).reshape(tail_count // page_size, page_size)
    tail_seen = (tail_spots[None] < tail_len[0][:, None, None])[:, :, None, None, None, :]
    tail_top, tail_total, tail_weights = block_stats(tail_scores, tail_seen)
    tail_numer = jnp.einsum(
        "sbikgt,sbtkd->sbikgd",
        tail_weights,
        tail_block_list[:, :, :, 1],
        preferred_element_type=jnp.float32,
    )
    fresh_scores = (
        jnp.einsum("sikgd,sjkd->sikgj", rotated_query, key_rot, preferred_element_type=jnp.float32)
        * score_scale
    )
    fresh_range = jnp.arange(fresh_count, dtype=jnp.int32)
    fresh_seen = (fresh_range[None, :] <= fresh_range[:, None])[None, :, None, None, :]
    fresh_top, fresh_total, fresh_weights = block_stats(fresh_scores, fresh_seen)
    fresh_numer = jnp.einsum(
        "sikgj,sjkd->sikgd", fresh_weights, value_new, preferred_element_type=jnp.float32
    )
    overall = jnp.maximum(
        jnp.maximum(jnp.max(page_top, axis=0), jnp.max(tail_top, axis=1)), fresh_top
    )
    page_factor = jnp.exp(page_top - overall[None])
    tail_factor = jnp.exp(tail_top - overall[:, None])
    fresh_factor = jnp.exp(fresh_top - overall)
    denominator = (
        jnp.sum(page_factor * page_total, axis=0)
        + jnp.sum(tail_factor * tail_total, axis=1)
        + fresh_factor * fresh_total
    )
    numerator = (
        jnp.sum(page_factor[..., None] * page_numer, axis=0)
        + jnp.sum(tail_factor[..., None] * tail_numer, axis=1)
        + fresh_factor[..., None] * fresh_numer
    )
    attn_rows = (
        (numerator / denominator[..., None])
        .astype(jnp.bfloat16)
        .reshape(row_count, head_count * HEAD_DIM)
    )
    attn_part = jnp.dot(attn_rows, out_weight, preferred_element_type=jnp.float32)
    layer_out, row_score = moe_call(
        flat_tokens, attn_part, routes.reshape(row_count, -1), norm_gains, router, expert_in,
        expert_out, score_weight,
    )
    return (
        layer_out.reshape(1, samples, fresh_count, model_width),
        row_score.reshape(1, samples, fresh_count),
    )


def solution(mesh):
    placed = (
        P("req", None, None, None),
        P(),
        P("req", None),
        P(),
        P(),
        P("req", None, None, "tp"),
        P("req", None, None, None, "tp"),
        P("req", None, None, None),
        P(),
        P(None, "tp"),
        P(None, None, "tp"),
        P("tp", None),
        P(),
        P("req", None, None, "tp"),
        P("req", "tp", None),
        P(),
    )
    return jax.shard_map(
        shards,
        mesh=mesh,
        in_specs=placed,
        out_specs=(P("req", None, None, None), P("req", None, None)),
        check_vma=False,
    )
```

```python
import jax
import jax.numpy as jnp
from jax import lax
from jax.experimental import pallas as pl
from jax.experimental.pallas import tpu as pltpu
from jax.sharding import PartitionSpec as P

EPSILON = 1e-05
ROPE_BASE = 10000.0
LOWEST = -1e30
MESH = pl.DeviceIdType.MESH
F32 = jnp.float32
BF16 = jnp.bfloat16


def iota(shape, dim):
    return lax.broadcasted_iota(jnp.int32, shape, dim)


def mm(a, b):
    return lax.dot_general(a, b, (((1,), (0,)), ((), ())), preferred_element_type=F32)


def mm_t(a, b):
    return lax.dot_general(a, b, (((1,), (1,)), ((), ())), preferred_element_type=F32)


def remote(src, dst, send_sem, recv_sem, req, tp):
    return pltpu.make_async_remote_copy(
        src_ref=src,
        dst_ref=dst,
        send_sem=send_sem,
        recv_sem=recv_sem,
        device_id=(req, tp),
        device_id_type=MESH,
    )


def spread_halves(values):
    high = values.astype(BF16)
    return high, (values - high.astype(F32)).astype(BF16)


def deinterleave(src_ref, dst_ref):
    row = iota((256, 256), 0)
    pick = (iota((256, 256), 1) == 2 * (row % 128) + row // 128).astype(BF16)
    for block in range(src_ref.shape[0] // 256):
        both = mm(pick, src_ref[pl.ds(block * 256, 256), :]).astype(BF16)
        dst_ref[pl.ds(block * 128, 128), 0:128] = both[:128]
        dst_ref[pl.ds(block * 128, 128), 128:256] = both[128:]


def rms(values, gain):
    return values * lax.rsqrt(jnp.mean(values * values, axis=-1, keepdims=True) + EPSILON) * gain


def exchange_start(slots, send_sem, recv_sem, req, tp):
    for step in (1, 3, 2):
        remote(
            slots.at[tp], slots.at[tp], send_sem.at[step], recv_sem.at[tp], req, (tp + step) % 4
        ).start()


def exchange_finish(slots, send_sem, recv_sem, req, tp):
    for step in (1, 3, 2):
        other = (tp + step) % 4
        copy = remote(slots.at[tp], slots.at[other], send_sem.at[step], recv_sem.at[other], req, other)
        copy.wait_recv()
    for step in (1, 3, 2):
        copy = remote(slots.at[tp], slots.at[tp], send_sem.at[step], recv_sem.at[tp], req, tp)
        copy.wait_send()
    return (
        slots[0].astype(F32) + slots[1].astype(F32) + slots[2].astype(F32) + slots[3].astype(F32)
    )


def route_tables(routes):
    column = iota((32, 32), 1)
    uses = jnp.zeros((32, 32), F32)
    for k in range(8):
        uses = uses + (routes[:, k : k + 1] == column).astype(F32)
    earlier = (iota((32, 32), 0) > column).astype(BF16)
    rank = mm(earlier, uses.astype(BF16))
    return uses, jnp.where(uses > 0, rank, -1.0).astype(BF16)


def spread_matrices(rank):
    repeat = (iota((256, 32), 0) // 8 == iota((256, 32), 1)).astype(BF16)
    slot = (iota((256, 32), 0) % 8).astype(F32)
    whole = (mm_t(repeat, rank) == slot).astype(F32).astype(BF16)
    slot2 = iota((256, 64), 0) % 8
    at_half = mm_t(repeat, jnp.concatenate([rank, rank], axis=0))
    half = (
        jnp.where(iota((256, 64), 1) // 32 == slot2 // 4, at_half, -1.0)
        == (8 + slot2 % 4).astype(F32)
    )
    return whole, half.astype(F32).astype(BF16)


def combine_matrices(rank, gates):
    repeat = (iota((256, 32), 0) // 8 == iota((256, 32), 1)).astype(BF16)
    at = mm_t(rank, repeat)
    gate_parts = [mm_t(part, repeat) for part in spread_halves(gates)]
    slot = iota((32, 256), 1) % 8
    chosen = [at == slot.astype(F32)]
    for h in range(2):
        chosen.append(jnp.where(slot // 4 == h, at, -1.0) == (8 + slot % 4).astype(F32))
    return [[jnp.where(pick, part, 0.0).astype(BF16) for part in gate_parts] for pick in chosen]


def moe_stage(req, tp, residual, routes_ref, gains_ref, router_ref, eout_ref, score_ref,
              out_ref, row_score_ref, win, out_buf, in_buf, ret_buf, back_buf, mix_slots,
              dsend, drecv, rsend, rrecv, lsem, msend, mrecv):
    z = req // 8
    xc = req % 8
    core = req % 2
    far = jnp.where(core == 0, 2, 6)
    hops = (0, 1, 7, far)

    uses, rank = route_tables(routes_ref[...])
    whole, half = spread_matrices(rank)
    normed = rms(residual.astype(F32), gains_ref[1:2, :]).astype(BF16)
    out_buf[:, :, 0:1024] = mm(whole, normed).reshape(32, 8, 1024).astype(BF16)
    stacked = jnp.concatenate([normed[:, :512], normed[:, 512:]], axis=0)
    out_buf[:, :, 1024:1536] = mm(half, stacked).reshape(32, 8, 512).astype(BF16)

    for g in (3, 2, 1, 0):
        to_z = (z + hops[g]) % 8
        base = (to_z % 4) * 8

        @pl.loop(1, 8)
        def _(i):
            other = (xc + i) % 8
            remote(
                out_buf.at[base + other], in_buf.at[g, xc], dsend.at[g, i], drecv.at[g, xc],
                to_z * 8 + other, tp,
            ).start()

        if g == 0:
            pltpu.make_async_copy(out_buf.at[base + xc], in_buf.at[0, xc], lsem.at[0]).start()
        else:
            remote(
                out_buf.at[base + xc], in_buf.at[g, xc], dsend.at[g, 0], drecv.at[g, xc],
                to_z * 8 + xc, tp,
            ).start()

    logits = mm_t(normed, router_ref[...])
    shown = jnp.where(uses > 0, logits, LOWEST)
    weights = jnp.where(uses > 0, jnp.exp(shown - jnp.max(shown, axis=-1, keepdims=True)), 0.0)
    gates = weights / jnp.sum(weights, axis=-1, keepdims=True)
    combine = combine_matrices(rank, gates)

    own_expert = (z % 4) * 8 + xc
    backs = (0, 7, 1, (8 - far) % 8)
    upper = iota((64, 1), 0) % 8 < 4

    for g in range(4):
        def from_z(other):
            if g < 3:
                return (z + backs[g]) % 8
            return (z + jnp.where(other % 2 == 0, 6, 2)) % 8

        if g == 0:
            pltpu.make_async_copy(out_buf.at[own_expert], in_buf.at[0, xc], lsem.at[0]).wait()

        @pl.loop(1 if g == 0 else 0, 8)
        def _(i):
            other = (xc + i) % 8
            remote(
                out_buf.at[0], in_buf.at[g, other], dsend.at[g, i], drecv.at[g, other], req, tp
            ).wait_recv()

        rows = in_buf[g].astype(F32)
        rows_a = rows[:, :, :1024].reshape(64, 1024).astype(BF16)
        rows_b = rows[:, :, 1024:].reshape(64, 512).astype(BF16)
        up_a = mm(rows_a, win[...])
        low = mm(rows_b, win[0:512, :])
        high = mm(rows_b, win[512:1024, :])
        mine = jnp.where(upper, low, high)
        swapped = jnp.where(upper, pltpu.roll(mine, 60, 0), pltpu.roll(mine, 4, 0))
        up_b = mine + swapped
        both = jnp.concatenate([up_a, up_b], axis=0)
        gate = both[:, :128]
        hidden = (gate / (1.0 + jnp.exp(-gate)) * both[:, 128:]).astype(BF16)
        result = mm(hidden, eout_ref[...])
        ret_buf[g, :, :, 0:1024] = result[:64].reshape(8, 8, 1024).astype(BF16)
        second = result[64:]
        ret_buf[g, :, :, 1024:1536] = (
            jnp.where(upper, second[:, :512], second[:, 512:]).reshape(8, 8, 512).astype(BF16)
        )

        if g == 0:
            pltpu.make_async_copy(ret_buf.at[0, xc], back_buf.at[own_expert], lsem.at[1]).start()

        @pl.loop(1 if g == 0 else 0, 8)
        def _(i):
            other = (xc + i) % 8
            remote(
                ret_buf.at[g, other], back_buf.at[own_expert], rsend.at[g, i],
                rrecv.at[own_expert], from_z(other) * 8 + other, tp,
            ).start()

    pltpu.make_async_copy(ret_buf.at[0, xc], back_buf.at[own_expert], lsem.at[1]).wait()

    @pl.loop(1, 32)
    def _(i):
        expert = (own_expert + i) % 32
        remote(
            ret_buf.at[0, 0], back_buf.at[expert], rsend.at[0, 0], rrecv.at[expert], req, tp
        ).wait_recv()

    back = back_buf[...].astype(F32)
    back_a = back[:, :, :1024].reshape(256, 1024).astype(BF16)
    back_b = back[:, :, 1024:].reshape(256, 512).astype(BF16)
    mix_b = [mm(combine[1 + h][0], back_b) + mm(combine[1 + h][1], back_b) for h in range(2)]
    mix = mm(combine[0][0], back_a) + mm(combine[0][1], back_a)
    mix = mix + jnp.concatenate(mix_b, axis=1)
    mix_slots[tp] = mix.astype(BF16)
    exchange_start(mix_slots, msend, mrecv, req, tp)

    for g in range(4):

        @pl.loop(1 if g == 0 else 0, 8)
        def _(i):
            remote(
                out_buf.at[0], in_buf.at[g, 0], dsend.at[g, i], drecv.at[g, 0], req, tp
            ).wait_send()
            remote(
                ret_buf.at[g, 0], back_buf.at[0], rsend.at[g, i], rrecv.at[0], req, tp
            ).wait_send()

    expert_mix = exchange_finish(mix_slots, msend, mrecv, req, tp)
    layer_out = (residual.astype(F32) + expert_mix).astype(BF16)
    out_ref[...] = layer_out
    final = rms(layer_out.astype(F32), gains_ref[2:3, :])
    row_score_ref[...] = jnp.sum(final * score_ref[...], axis=-1, keepdims=True)


def moe_scratch():
    dma = pltpu.SemaphoreType.DMA
    return [
        pltpu.VMEM((1024, 256), BF16),
        pltpu.VMEM((32, 8, 1536), BF16),
        pltpu.VMEM((4, 8, 8, 1536), BF16),
        pltpu.VMEM((4, 8, 8, 1536), BF16),
        pltpu.VMEM((32, 8, 1536), BF16),
        pltpu.VMEM((4, 32, 1024), BF16),
        dma((4, 8)),
        dma((4, 8)),
        dma((4, 8)),
        dma((32,)),
        dma((2,)),
        dma((4,)),
        dma((4,)),
    ]


def rotate(values, cosine, sine):
    width = values.shape[1]
    first = iota((1, width), 1) % 64 < 32
    partner = jnp.where(first, pltpu.roll(values, width - 32, 1), pltpu.roll(values, 32, 1))
    return values * cosine + partner * sine


def masked_softmax(scores, visible):
    top = jnp.max(jnp.where(visible, scores, LOWEST), axis=-1, keepdims=True)
    weights = jnp.where(visible, jnp.exp(jnp.where(visible, scores - top, 0.0)), 0.0)
    return top, jnp.sum(weights, axis=-1, keepdims=True), weights


def shift_lanes(weights):
    parts = [
        pltpu.roll(weights[:, at : at + 128], 1, 1) for at in range(0, weights.shape[1], 128)
    ]
    return jnp.concatenate(parts, axis=1).astype(BF16)


def as_row(column):
    square = iota((128, 128), 0) == iota((128, 128), 1)
    return jnp.sum(jnp.where(square, column, 0.0), axis=0, keepdims=True)


def z_order(k):
    return (k + 1) // 2 if k % 2 else (8 - k // 2) % 8


def merge_weights(stats):
    top = stats[0][0]
    for other, _ in stats[1:]:
        top = jnp.maximum(top, other)
    shares = [jnp.exp(part - top) * total for part, total in stats]
    total = shares[0]
    for share in shares[1:]:
        total = total + share
    scale = 1.0 / jnp.maximum(total, 1e-30)
    return top, total, [share * scale for share in shares]


def widen(columns, at):
    return jnp.where(iota((64, 128), 1) < 64, columns[:64, at : at + 1], columns[64:, at : at + 1])


def three_parts(values):
    high = values.astype(BF16)
    rest = values - high.astype(F32)
    middle = rest.astype(BF16)
    return high, middle, (rest - middle.astype(F32)).astype(BF16)


def query_sends(req, tp, q_all, qz_s, qz_r):
    z, x, c = req // 8, req % 8 // 2, req % 2
    for dz in (4, 3, 5, 2, 6, 1, 7):
        remote(
            q_all.at[z, x, c], q_all.at[z, x, c], qz_s.at[dz], qz_r.at[z],
            (z + dz) % 8 * 8 + x * 2 + c, tp,
        ).start()


def query_forward_x(req, tp, q_all, qz_r, qx_s, qx_r, qc_s, qc_r):
    z, x, c = req // 8, req % 8 // 2, req % 2
    for k in range(8):
        zz = (z + z_order(k)) % 8
        if k:
            remote(
                q_all.at[z, x, c], q_all.at[zz, x, c], qx_s.at[0, 0], qz_r.at[zz], req, tp
            ).wait_recv()
        for dx in (2, 1, 3):
            remote(
                q_all.at[zz, x, c], q_all.at[zz, x, c], qx_s.at[zz, dx], qx_r.at[zz, x],
                z * 8 + (x + dx) % 4 * 2 + c, tp,
            ).start()
        remote(
            q_all.at[zz, x, c], q_all.at[zz, x, c], qc_s.at[zz, x], qc_r.at[zz, x],
            z * 8 + x * 2 + 1 - c, tp,
        ).start()


def query_forward_core(req, tp, q_all, qx_s, qx_r, qc_s, qc_r):
    z, x, c = req // 8, req % 8 // 2, req % 2
    for k in range(8):
        zz = (z + z_order(k)) % 8
        for dx in (1, 3, 2):
            xx = (x + dx) % 4
            remote(
                q_all.at[z, x, c], q_all.at[zz, xx, c], qx_s.at[0, 0], qx_r.at[zz, xx], req, tp
            ).wait_recv()
            remote(
                q_all.at[zz, xx, c], q_all.at[zz, xx, c], qc_s.at[zz, xx], qc_r.at[zz, xx],
                z * 8 + x * 2 + 1 - c, tp,
            ).start()


def query_finish(req, tp, q_all, qz_s, qx_s, qc_s, qc_r):
    z, x, c = req // 8, req % 8 // 2, req % 2

    @pl.loop(0, 32)
    def _(i):
        remote(
            q_all.at[z, x, c], q_all.at[i // 4, i % 4, 1 - c], qx_s.at[0, 0],
            qc_r.at[i // 4, i % 4], req, tp,
        ).wait_recv()


def query_drain(req, tp, q_all, qz_s, qx_s, qc_s):
    z, x, c = req // 8, req % 8 // 2, req % 2

    def drain(sem):
        remote(q_all.at[z, x, c], q_all.at[z, x, c], sem, sem, req, tp).wait_send()

    @pl.loop(1, 8)
    def _(i):
        drain(qz_s.at[i])

    @pl.loop(0, 32)
    def _(i):
        drain(qc_s.at[i // 4, i % 4])

    @pl.loop(0, 24)
    def _(i):
        drain(qx_s.at[i // 3, 1 + i % 3])


def page_partials(meta, q_flat, pages, slot_out, slot_stats):
    lane = iota((128, 256), 1)
    even = lane % 2 == 0
    left = iota((64, 128), 1) < 64

    def one(v):
        query = q_flat[meta[v]].astype(F32)
        split = jnp.concatenate(
            [jnp.where(left, query, 0.0), jnp.where(left, 0.0, query)], axis=0
        ).astype(BF16)
        rows = pages[v]
        top, total, weights = masked_softmax(
            mm_t(split, rows), even & (lane < 2 * meta[32 + v])
        )
        numer = mm(shift_lanes(weights), rows) / jnp.maximum(total, 1e-30)
        slot_out[v] = jnp.where(left, numer[:64], numer[64:]).astype(BF16)
        slot_stats[v] = jnp.concatenate([as_row(top), as_row(total)], axis=1)

    @pl.loop(0, 8)
    def _(step):
        for at in range(4):
            one(step * 4 + at)


def partial_exchange(req, tp, meta, slot_out, slot_stats, send_o, send_s, ex_o, ex_s,
                     es, er, lsem):
    z, xc = req // 8, req % 8
    empty = jnp.where(iota((1, 256), 1) < 128, LOWEST, 0.0)

    def fill(other):
        @pl.loop(0, 8)
        def _(zz):
            slot = meta[64 + zz * 8 + other]
            held = jnp.maximum(slot, 0)
            send_o[other, zz] = slot_out[held]
            send_s[other, pl.ds(zz, 1), :] = jnp.where(slot >= 0, slot_stats[held], empty)

    for step in (4, 5, 3, 2, 6, 7, 1):
        other = (xc + step) % 8
        fill(other)
        remote(send_o.at[other], ex_o.at[xc], es.at[0, step], er.at[0, xc], z * 8 + other, tp).start()
        remote(send_s.at[other], ex_s.at[xc], es.at[1, step], er.at[1, xc], z * 8 + other, tp).start()
    fill(xc)
    pltpu.make_async_copy(send_o.at[xc], ex_o.at[xc], lsem.at[0]).start()
    pltpu.make_async_copy(send_s.at[xc], ex_s.at[xc], lsem.at[1]).start()


def partial_merge(req, tp, send_o, send_s, ex_o, ex_s, comb_o, comb_s, ex2_o, ex2_s,
                  er, es, lsem, fs, fr):
    z, xc = req // 8, req % 8
    pltpu.make_async_copy(send_o.at[xc], ex_o.at[xc], lsem.at[0]).wait()
    pltpu.make_async_copy(send_s.at[xc], ex_s.at[xc], lsem.at[1]).wait()

    @pl.loop(1, 8)
    def _(step):
        other = (xc + step) % 8
        remote(send_o.at[0], ex_o.at[other], es.at[0, 0], er.at[0, other], req, tp).wait_recv()
        remote(send_s.at[0], ex_s.at[other], es.at[1, 0], er.at[1, other], req, tp).wait_recv()

    stats = [(ex_s[src][:, :128], ex_s[src][:, 128:]) for src in range(8)]
    top, total, shares = merge_weights(stats)
    columns = jnp.concatenate(shares + [jnp.zeros((64, 128), F32)], axis=0).T
    for zz in range(8):
        merged = jnp.zeros((64, 128), F32)
        for src in range(8):
            merged = merged + ex_o[src, zz].astype(F32) * widen(columns, src * 8 + zz)
        comb_o[zz] = merged.astype(BF16)
        comb_s[zz, :, 0:128] = top[zz : zz + 1]
        comb_s[zz, :, 128:256] = total[zz : zz + 1]
    for dz in (4, 3, 5, 2, 6, 1, 7):
        to_z = (z + dz) % 8
        remote(comb_o.at[to_z], ex2_o.at[z], fs.at[0, dz], fr.at[0, z], to_z * 8 + xc, tp).start()
        remote(comb_s.at[to_z], ex2_s.at[z], fs.at[1, dz], fr.at[1, z], to_z * 8 + xc, tp).start()
    pltpu.make_async_copy(comb_o.at[z], ex2_o.at[z], lsem.at[2]).start()
    pltpu.make_async_copy(comb_s.at[z], ex2_s.at[z], lsem.at[3]).start()


def prefix_finish(req, tp, comb_o, comb_s, ex2_o, ex2_s, lsem, fs, fr):
    z, xc = req // 8, req % 8
    pltpu.make_async_copy(comb_o.at[z], ex2_o.at[z], lsem.at[2]).wait()
    pltpu.make_async_copy(comb_s.at[z], ex2_s.at[z], lsem.at[3]).wait()

    @pl.loop(1, 8)
    def _(dz):
        other = (z + dz) % 8
        remote(comb_o.at[0], ex2_o.at[other], fs.at[0, 0], fr.at[0, other], req, tp).wait_recv()
        remote(comb_s.at[0], ex2_s.at[other], fs.at[1, 0], fr.at[1, other], req, tp).wait_recv()

    stats = [(ex2_s[src][:, :128], ex2_s[src][:, 128:]) for src in range(8)]
    top, total, shares = merge_weights(stats)
    columns = jnp.concatenate(shares + [top, total, jnp.zeros((118, 128), F32)], axis=0).T
    merged = jnp.zeros((64, 128), F32)
    for src in range(8):
        merged = merged + ex2_o[src].astype(F32) * widen(columns, src)
    return widen(columns, 8), widen(columns, 9), merged


def partial_drain(req, tp, send_o, send_s, comb_o, comb_s, es, fs):
    @pl.loop(1, 8)
    def _(i):
        remote(send_o.at[0], send_o.at[0], es.at[0, i], es.at[0, i], req, tp).wait_send()
        remote(send_s.at[0], send_s.at[0], es.at[1, i], es.at[1, i], req, tp).wait_send()
        remote(comb_o.at[0], comb_o.at[0], fs.at[0, i], fs.at[0, i], req, tp).wait_send()
        remote(comb_s.at[0], comb_s.at[0], fs.at[1, i], fs.at[1, i], req, tp).wait_send()


def sample_queries(query_pair):
    token = (iota((128, 32), 0) // 4 == iota((128, 32), 1)).astype(BF16)
    rows = mm(token, query_pair)
    row = iota((128, 128), 0)
    mine = jnp.where(row % 2 == 0, rows[:, :128], rows[:, 128:])
    return jnp.where(iota((128, 128), 1) // 64 == row % 4 // 2, mine, 0.0)


def tail_partials(meta, queries, tail, tail_num, tail_top, tail_total, begin, end):
    lane = iota((8, 1024), 1)
    even = lane % 2 == 0

    def one(s):
        rows = tail[s]
        query = queries[pl.ds(pl.multiple_of(s * 8, 8), 8), :].astype(BF16)
        top, total, weights = masked_softmax(
            mm_t(query, rows), even & (lane < 2 * meta[128 + s])
        )
        at = pl.ds(pl.multiple_of(s * 8, 8), 8)
        tail_num[at, :] = mm(shift_lanes(weights), rows)
        tail_top[at, :] = jnp.broadcast_to(top, (8, 128))
        tail_total[at, :] = jnp.broadcast_to(total, (8, 128))

    @pl.loop(begin // 4, end // 4)
    def _(step):
        for at in range(4):
            one(step * 4 + at)


def own_finish(queries, key_rot, value_new, tail_num, tail_top, tail_total):
    row, col = iota((128, 32), 0), iota((128, 32), 1)
    visible = (row // 8 == col // 2) & (col % 2 <= row % 8 // 4)
    top_f, total_f, weights = masked_softmax(mm_t(queries.astype(BF16), key_rot), visible)
    numer_f = mm(weights.astype(BF16), value_new)
    top = jnp.maximum(tail_top[...], top_f)
    share_t = jnp.exp(tail_top[...] - top)
    share_f = jnp.exp(top_f - top)
    total = share_t * tail_total[...] + share_f * total_f
    numer = (share_t * tail_num[...] + share_f * numer_f) / total
    row = iota((128, 128), 0)
    own = iota((128, 128), 1) // 64 == row % 4 // 2
    pick_row, pick_col = iota((64, 128), 0), iota((64, 128), 1)
    pick = (pick_col // 4 == pick_row % 32) & (pick_col % 2 == pick_row // 32)
    pick = pick.astype(F32).astype(BF16)

    def compact(values, cut):
        parts = cut(jnp.where(own, values, 0.0))
        out = mm(pick, parts[0])
        for part in parts[1:]:
            out = out + mm(pick, part)
        return out

    return compact(top, three_parts), compact(total, three_parts), compact(numer, spread_halves)


def layer_kernel(
    meta, tok_ref, cos_ref, sin_ref, routes_ref, gains_ref, router_ref, score_ref,
    wq_hbm, wkv_hbm, wo_hbm, pages_hbm, tail_hbm, ein_hbm, eout_hbm,
    out_ref, row_score_ref,
    wq, wkv, wo, pages, tail, ein, eout, loads, wkv_flat, q_all, queries,
    tail_num, tail_top, tail_total, slot_out, slot_stats, send_o, send_s, ex_o, ex_s,
    comb_o, comb_s, ex2_o, ex2_s,
    qz_s, qz_r, qx_s, qx_r, qc_s, qc_r, es, er, fs, fr, plsem,
    attn_slots, asend, arecv, win, *rest
):
    req = lax.axis_index("req")
    tp = lax.axis_index("tp")
    z, x, c = req // 8, req % 8 // 2, req % 2
    barrier = pltpu.get_barrier_semaphore()
    for step in (1, 2, 3):
        pl.semaphore_signal(barrier, 1, device_id=(req, (tp + step) % 4), device_id_type=MESH)

    @pl.loop(1, 64)
    def _(i):
        pl.semaphore_signal(barrier, 1, device_id=((req + i) % 64, tp), device_id_type=MESH)

    moves = [
        pltpu.make_async_copy(src, dst, loads.at[i])
        for i, (src, dst) in enumerate(
            [(wq_hbm, wq), (wkv_hbm, wkv), (tail_hbm, tail), (pages_hbm, pages), (wo_hbm, wo),
             (ein_hbm, ein), (eout_hbm, eout)]
        )
    ]
    for move in moves:
        move.start()

    normed = rms(tok_ref[...].astype(F32), gains_ref[0:1, :]).astype(BF16)
    cosine, sine = cos_ref[...], sin_ref[...]
    moves[0].wait()
    query = rotate(
        mm(normed, wq[...]),
        jnp.concatenate([cosine, cosine], axis=1),
        jnp.concatenate([sine, sine], axis=1),
    )
    query = query.astype(BF16).astype(F32) * 0.125
    left = iota((32, 128), 1) < 64
    low, high = query[:, :128], query[:, 128:]
    first = jnp.where(left, low, pltpu.roll(high, 64, 1))
    second = jnp.where(left, pltpu.roll(low, 64, 1), high)
    q_all[z, x, c] = jnp.concatenate([first, second], axis=0).astype(BF16)
    pl.semaphore_wait(barrier, 66)
    query_sends(req, tp, q_all, qz_s, qz_r)

    moves[1].wait()
    deinterleave(wkv, wkv_flat)
    key_value = mm(normed, wkv_flat[...])
    key_rot = rotate(key_value[:, :128], cosine, sine).astype(BF16)
    value_new = key_value[:, 128:].astype(BF16)
    queries[...] = sample_queries(jnp.concatenate([first, second], axis=1).astype(BF16))
    moves[2].wait()

    query_forward_x(req, tp, q_all, qz_r, qx_s, qx_r, qc_s, qc_r)
    tail_partials(meta, queries, tail, tail_num, tail_top, tail_total, 0, 12)
    query_forward_core(req, tp, q_all, qx_s, qx_r, qc_s, qc_r)
    moves[3].wait()
    query_finish(req, tp, q_all, qz_s, qx_s, qc_s, qc_r)

    page_partials(meta, q_all.reshape(64, 64, 128), pages, slot_out, slot_stats)
    partial_exchange(req, tp, meta, slot_out, slot_stats, send_o, send_s, ex_o, ex_s, es, er, plsem)
    tail_partials(meta, queries, tail, tail_num, tail_top, tail_total, 12, 16)
    own_top, own_total, own_numer = own_finish(
        queries[...], key_rot, value_new, tail_num, tail_top, tail_total
    )
    moves[4].wait()
    moves[5].wait()
    moves[6].wait()
    deinterleave(ein, win)
    query_drain(req, tp, q_all, qz_s, qx_s, qc_s)
    partial_merge(req, tp, send_o, send_s, ex_o, ex_s, comb_o, comb_s, ex2_o, ex2_s,
                  er, es, plsem, fs, fr)
    top, total, numer = prefix_finish(req, tp, comb_o, comb_s, ex2_o, ex2_s, plsem, fs, fr)
    most = jnp.maximum(top, own_top)
    share = jnp.exp(top - most) * total
    own_share = jnp.exp(own_top - most) * own_total
    attn = ((share * numer + own_share * own_numer) / (share + own_share)).astype(BF16)
    out_weight = jnp.concatenate([wo[0:64], wo[128:192], wo[64:128], wo[192:256]], axis=0)
    part = mm(jnp.concatenate([attn[:32], attn[32:]], axis=1), out_weight)
    attn_slots[tp] = part.astype(BF16)
    exchange_start(attn_slots, asend, arecv, req, tp)
    partial_drain(req, tp, send_o, send_s, comb_o, comb_s, es, fs)
    attn_out = exchange_finish(attn_slots, asend, arecv, req, tp)
    residual = (tok_ref[...].astype(F32) + attn_out).astype(BF16)
    moe_stage(req, tp, residual, routes_ref, gains_ref, router_ref, eout, score_ref,
              out_ref, row_score_ref, win, *rest)


def layer_call(meta, *arrays):
    dma = pltpu.SemaphoreType.DMA
    vmem = pl.BlockSpec(memory_space=pltpu.VMEM)
    anywhere = pl.BlockSpec(memory_space=pl.ANY)
    buffers = [
        pltpu.VMEM((1024, 256), BF16),
        pltpu.VMEM((2048, 128), BF16),
        pltpu.VMEM((256, 1024), BF16),
        pltpu.VMEM((32, 256, 128), BF16),
        pltpu.VMEM((16, 1024, 128), BF16),
        pltpu.VMEM((2048, 128), BF16),
        pltpu.VMEM((128, 1024), BF16),
        dma((7,)),
        pltpu.VMEM((1024, 256), BF16),
        pltpu.VMEM((8, 4, 2, 64, 128), BF16),
        pltpu.VMEM((128, 128), F32),
        pltpu.VMEM((128, 128), F32),
        pltpu.VMEM((128, 128), F32),
        pltpu.VMEM((128, 128), F32),
        pltpu.VMEM((32, 64, 128), BF16),
        pltpu.VMEM((32, 1, 256), F32),
        pltpu.VMEM((8, 8, 64, 128), BF16),
        pltpu.VMEM((8, 8, 256), F32),
        pltpu.VMEM((8, 8, 64, 128), BF16),
        pltpu.VMEM((8, 8, 256), F32),
        pltpu.VMEM((8, 64, 128), BF16),
        pltpu.VMEM((8, 1, 256), F32),
        pltpu.VMEM((8, 64, 128), BF16),
        pltpu.VMEM((8, 1, 256), F32),
        dma((8,)),
        dma((8,)),
        dma((8, 4)),
        dma((8, 4)),
        dma((8, 4)),
        dma((8, 4)),
        dma((2, 8)),
        dma((2, 8)),
        dma((2, 8)),
        dma((2, 8)),
        dma((4,)),
        pltpu.VMEM((4, 32, 1024), BF16),
        dma((4,)),
        dma((4,)),
    ]
    return pl.pallas_call(
        layer_kernel,
        out_shape=(
            jax.ShapeDtypeStruct((32, 1024), BF16),
            jax.ShapeDtypeStruct((32, 1), F32),
        ),
        in_specs=[pl.BlockSpec(memory_space=pltpu.SMEM)] + [vmem] * 7 + [anywhere] * 7,
        out_specs=(vmem, vmem),
        scratch_shapes=buffers + moe_scratch(),
        compiler_params=pltpu.CompilerParams(
            collective_id=0, has_side_effects=True, vmem_limit_bytes=48 * 1024 * 1024
        ),
    )(meta, *arrays)


def shards(
    tokens_new, prefix_len, tail_len, pool_home, pool_page, slot_page_cache, tail_cache, routes,
    norm_gains, query_weight, key_value_weight, out_weight, router, expert_in, expert_out,
    score_weight,
):
    req = lax.axis_index("req")
    home = lax.dynamic_slice(pool_home, (req * 32,), (32,))
    page = lax.dynamic_slice(pool_page, (req * 32,), (32,))
    held = home[None, :] == jnp.arange(64, dtype=jnp.int32)[:, None]
    slot_of = jnp.sum(held * (jnp.arange(32, dtype=jnp.int32) + 1)[None, :], axis=1) - 1
    lengths = jnp.sum(jnp.where(held, prefix_len[:, None], 0), axis=0)
    meta = jnp.concatenate([home, lengths - page * 128, slot_of, tail_len[0]])

    fresh = jnp.arange(2, dtype=jnp.int32)
    positions = (prefix_len[req] + tail_len[0][:, None] + fresh[None, :]).reshape(32)
    frequency = ROPE_BASE ** (-jnp.arange(32, dtype=jnp.float32) / 32)
    angles = positions.astype(jnp.float32)[:, None] * jnp.tile(frequency, 4)[None, :]
    sign = jnp.where(jnp.arange(128) % 64 < 32, -1.0, 1.0).astype(jnp.float32)
    layer_out, row_score = layer_call(
        meta, tokens_new.reshape(32, 1024), jnp.cos(angles), jnp.sin(angles) * sign,
        routes.reshape(32, 8), norm_gains, router.T, score_weight[None],
        query_weight, key_value_weight.reshape(2048, 128), out_weight,
        slot_page_cache.reshape(32, 256, 128), tail_cache.reshape(16, 1024, 128),
        expert_in.reshape(2048, 128), expert_out[0],
    )
    return layer_out.reshape(1, 16, 2, 1024), row_score.reshape(1, 16, 2)


def solution(mesh):
    placed = (
        P("req", None, None, None),
        P(),
        P("req", None),
        P(),
        P(),
        P("req", None, None, "tp"),
        P("req", None, None, None, "tp"),
        P("req", None, None, None),
        P(),
        P(None, "tp"),
        P(None, None, "tp"),
        P("tp", None),
        P(),
        P("req", None, None, "tp"),
        P("req", "tp", None),
        P(),
    )
    return jax.shard_map(
        shards,
        mesh=mesh,
        in_specs=placed,
        out_specs=(P("req", None, None, None), P("req", None, None)),
        check_vma=False,
    )
```
